256 devices in a mesh: pipe: 8 (over y, x_lo), expert: 32 (over x_hi, z, core).
Axes of the slice: x: 4 (x_hi: 2, x_lo: 2; x = x_hi * 2 + x_lo), y: 4, z: 8, core: 2. Of those that a mesh axis runs over, the one named last changes fastest.
Arguments:
- tokens_in: bfloat16 [2, 2560, 2048], P(None, 'expert'), may hold values from -6 to 6
- out_grad: bfloat16 [2, 2560, 2048], P(None, 'expert'), may hold values from -6 to 6
- routes: int32 [8, 2, 2560, 1], P(None, None, 'expert'), may hold values from 0 to 31; in each aligned block of 80 rows (0 to 79, 80 to 159, ..., all dimensions but the last counted through in order) at most 3 rows name the same one
- router: bfloat16 [8, 2048, 32], P('pipe'), may hold values from -0.125 to 0.125
- norm_gain: bfloat16 [8, 2048], P('pipe'), may hold values from 0.5 to 1.5
- w_in: bfloat16 [8, 32, 2048, 1024], P('pipe', 'expert'), may hold values from -0.125 to 0.125
- w_out: bfloat16 [8, 32, 512, 2048], P('pipe', 'expert'), may hold values from -0.25 to 0.25
Outputs:
- grad_in: bfloat16 [8, 32, 2048, 1024], P('pipe', 'expert')
- grad_out: bfloat16 [8, 32, 512, 2048], P('pipe', 'expert')
The draws below stay inside these ranges and needn't reach their ends.
Inputs may be any that keep to these rules, and one draw needn't show every extreme that they name: `routes`: in each aligned block of 80 rows (one device's tokens of one layer and microbatch) no expert is named by more than 3 tokens; a token's 1 ids differ.
All inputs are finite; a program needn't handle non-finite values.
Results may differ from the reference program's by a relative error of at most 0.029.
Values may be sent and summed in bfloat16 or wider, within the bound.
A program may use at most 128 MiB of HBM per device.

```python
import math
import jax
import jax.numpy as jnp
import numpy as np
from jax import lax

D = 2048
FW = 512
TOPK = 1
MICRO = 2
TOK_DEV = 80
LAYERS = 8
EXPERTS = 32
TOKENS = 2560
CAP = 3
N_EXPERT = 32


def block_levels(stream_key, shape, split, least, largest):
    level = 1.0
    for axis_at, shards_of in split:
        draws = jax.random.uniform(jax.random.fold_in(jax.random.fold_in(stream_key, 6), axis_at), (shards_of,), jnp.float32, least / len(split), largest / len(split))
        level = level * jnp.repeat(jnp.exp(draws), shape[axis_at] // shards_of).reshape((-1,) + (1,) * (len(shape) - 1 - axis_at))
    return level


def shared_out(key, own, number, rows, number_of, top, bound, skew):
    sequence = jax.random.permutation(key, number_of)
    crowded, common = load_shares(number_of, rows * top, bound, skew, True), load_shares(number_of, rows * top, bound, skew, False)
    places = jnp.arange(number_of)

    def named(lengths, turn):
        used = int((lengths > 0).sum())
        fixed = max(1, used // 4)
        passed = fixed + (places - fixed + turn * (used - fixed)) % max(1, number_of - fixed)
        return jnp.zeros((number_of,), jnp.int32).at[sequence[jnp.where(places < fixed, places, passed)]].set(jnp.asarray(lengths, jnp.int32))

    lengths = jnp.where(number % 4 == 0, named(crowded, number // 4), named(common, number - number // 4 - 1))
    mixed = jax.random.permutation(jax.random.fold_in(own, 3), number_of)
    giver, taker = mixed[0:number_of // 2 * 2:2], mixed[1:number_of // 2 * 2:2]
    slack = jnp.minimum(lengths[giver] - 1, bound - lengths[taker]) // 2
    slack = jnp.where((giver == sequence[0]) | (taker == sequence[0]) | (lengths[taker] == 0), 0, jnp.maximum(slack, 0))
    passed = jax.random.randint(jax.random.fold_in(own, 4), (number_of // 2,), 0, 1 << 20) % (slack + 1)
    lengths = lengths.at[giver].add(-passed).at[taker].add(passed)
    labels = jnp.searchsorted(jnp.cumsum(lengths), jnp.arange(rows * top), side="right").astype(jnp.int32)
    listing = labels.reshape(top, rows).T
    listing = listing[jax.random.permutation(jax.random.fold_in(own, 1), rows)]
    turn = jax.random.randint(jax.random.fold_in(own, 2), (rows, 1), 0, top)
    return jnp.take_along_axis(listing, (jnp.arange(top)[None, :] + turn) % top, axis=1)


def load_shares(number_of, total, most, slope, full):
    loads = [(1 << 20) // math.isqrt(grade ** slope) + 1 for grade in range(1, number_of + 1)]
    largest = most if full else min(most, max(-(-total // number_of), total * loads[0] // sum(loads)))
    least = 1 if total - largest >= number_of - 1 else 0
    counts, surplus = [largest] + [least] * (number_of - 1), total - largest - least * (number_of - 1)
    while surplus > 0:
        candidates = [i for i in range(1, number_of) if counts[i] < largest] or [i for i in range(1, number_of) if counts[i] < most]
        mass, left = sum([loads[i] for i in candidates]), surplus
        for i in candidates:
            extra = min(most - counts[i], max(1, left * loads[i] // mass), surplus)
            counts[i] = counts[i] + extra
            surplus = surplus - extra
    return np.array(counts)


def bell_draw(stream_key, shape, scale, bound, split=(), held_as=jnp.bfloat16):
    drawn = scale * jax.random.normal(stream_key, shape, jnp.float32)
    if split:
        drawn = drawn * block_levels(stream_key, shape, split, -0.22, 0.18)
    return jnp.clip(drawn, -bound, bound).astype(held_as)


def setup_inputs(seed: int = 0) -> dict:
    key_list = jax.random.split(jax.random.key(seed), 8)
    tokens_in = bell_draw(key_list[0], (MICRO, TOKENS, D), 1.0, 6.0, ((1, 32),))
    out_grad = bell_draw(key_list[1], (MICRO, TOKENS, D), 1.0, 6.0, ((1, 32),))
    routes_keys = jax.random.split(jax.random.fold_in(key_list[2], 1), LAYERS * MICRO * TOKENS // TOK_DEV)
    routes_turns = jax.random.permutation(jax.random.fold_in(key_list[2], 3), LAYERS * MICRO * TOKENS // TOK_DEV)
    routes = jax.vmap(lambda own, number: shared_out(jax.random.fold_in(key_list[2], 2), own, number, TOK_DEV, EXPERTS, TOPK, CAP, 1))(routes_keys, routes_turns).reshape((LAYERS, MICRO, TOKENS, TOPK))
    router = bell_draw(key_list[3], (LAYERS, D, EXPERTS), D ** -0.5, 0.125, ((0, 8),))
    norm_gain = jnp.clip(1.0 + 0.1 * jax.random.normal(key_list[4], (LAYERS, D), jnp.float32), 0.5, 1.5).astype(jnp.bfloat16)
    w_in = bell_draw(key_list[5], (LAYERS, EXPERTS, D, 2 * FW), D ** -0.5, 0.125, ((0, 8), (1, 32)))
    w_out = bell_draw(key_list[6], (LAYERS, EXPERTS, FW, D), FW ** -0.5, 0.25, ((0, 8), (1, 32)))
    return dict(tokens_in=tokens_in, out_grad=out_grad, routes=routes, router=router, norm_gain=norm_gain, w_in=w_in, w_out=w_out)


epsilon = 1e-06

def normalize(hidden, gain_row):
    values = hidden.astype(jnp.float32)
    inverse = lax.rsqrt(lax.optimization_barrier(jnp.mean(values * values, axis=-1, keepdims=True)) + epsilon)
    scaled = values * inverse
    normed = (scaled * gain_row.astype(jnp.float32)).astype(jnp.bfloat16)
    return (normed, scaled, inverse)

def router_gates(normed, router_cols, route_ids):
    logits_all = jnp.dot(normed, router_cols, preferred_element_type=jnp.float32)
    picked = route_ids[:, :, None] == jnp.arange(router_cols.shape[1], dtype=jnp.int32)[None, None, :]
    logits = lax.optimization_barrier(jnp.sum(jnp.where(picked, logits_all[:, None, :], 0.0), axis=-1))
    return (jax.nn.sigmoid(logits), picked)

def slot_owners(positions, slot_count):
    pair_count = positions.shape[0]
    owners = jnp.zeros((slot_count,), jnp.int32).at[positions].set(jnp.arange(pair_count, dtype=jnp.int32))
    filled = jnp.zeros((slot_count,), jnp.int32).at[positions].set(1)
    return (owners, filled > 0)

def to_slots(source, index_table, filled, slot_shape):
    gathered = source[index_table]
    mask_shape = (filled.shape[0],) + (1,) * (gathered.ndim - 1)
    chosen = jnp.where(filled.reshape(mask_shape), gathered, jnp.zeros((), source.dtype))
    return chosen.reshape(slot_shape)

def expert_forward(token_rows, weight_in, weight_out):
    inner_width = weight_out.shape[0]
    joined = jnp.dot(token_rows, weight_in, preferred_element_type=jnp.float32)
    gate_part = joined[:, :inner_width]
    activated = (gate_part * jax.nn.sigmoid(gate_part) * joined[:, inner_width:]).astype(jnp.bfloat16)
    return jnp.dot(activated, weight_out, preferred_element_type=jnp.float32).astype(jnp.bfloat16)

def expert_backward(token_rows, upstream, gate_share, weight_in, weight_out):
    inner_width = weight_out.shape[0]
    joined = jnp.dot(token_rows, weight_in, preferred_element_type=jnp.float32)
    gate_part = joined[:, :inner_width]
    up_part = joined[:, inner_width:]
    sigmoid_gate = jax.nn.sigmoid(gate_part)
    silu_gate = gate_part * sigmoid_gate
    activated = (silu_gate * up_part).astype(jnp.bfloat16)
    produced = jnp.dot(activated, weight_out, preferred_element_type=jnp.float32).astype(jnp.bfloat16)
    upstream_f = upstream.astype(jnp.float32)
    share_grad = lax.optimization_barrier(jnp.sum(produced.astype(jnp.float32) * upstream_f, axis=-1))
    scaled_grad = (gate_share.astype(jnp.float32)[:, None] * upstream_f).astype(jnp.bfloat16)
    act_grad = jnp.dot(scaled_grad, weight_out.T, preferred_element_type=jnp.float32)
    gate_grad = act_grad * up_part * sigmoid_gate * (1.0 + gate_part * (1.0 - sigmoid_gate))
    up_grad = act_grad * silu_gate
    joined_grad = jnp.concatenate([gate_grad, up_grad], axis=-1).astype(jnp.bfloat16)
    rows_grad = jnp.dot(joined_grad, weight_in.T, preferred_element_type=jnp.float32).astype(jnp.bfloat16)
    grad_in = jnp.dot(token_rows.T, joined_grad, preferred_element_type=jnp.float32)
    grad_out = jnp.dot(activated.T, scaled_grad, preferred_element_type=jnp.float32)
    return (rows_grad, share_grad, grad_in, grad_out)

def combine(hidden, gate_probs, pair_outputs):
    shares = lax.optimization_barrier(gate_probs.astype(jnp.bfloat16)).astype(jnp.float32)
    mixed = lax.optimization_barrier(jnp.sum(shares[:, :, None] * pair_outputs.astype(jnp.float32), axis=1))
    return (hidden.astype(jnp.float32) + mixed).astype(jnp.bfloat16)

def token_backward(upstream, scaled, inverse, gain_row, router_cols, gate_probs, picked, pair_grads, pair_shares):
    logit_grad = pair_shares.astype(jnp.float32) * gate_probs * (1.0 - gate_probs)
    spread = lax.optimization_barrier(jnp.sum(jnp.where(picked, logit_grad[:, :, None], 0.0), axis=1))
    normed_grad = lax.optimization_barrier(jnp.sum(pair_grads.astype(jnp.float32), axis=1)) + jnp.dot(spread, router_cols.astype(jnp.float32).T, precision=lax.Precision.HIGHEST)
    gained = normed_grad * gain_row.astype(jnp.float32)
    centred = gained - scaled * lax.optimization_barrier(jnp.mean(gained * scaled, axis=-1, keepdims=True))
    return (upstream.astype(jnp.float32) + inverse * centred).astype(jnp.bfloat16)

def positions_of(route_ids):
    blocks = route_ids.reshape(N_EXPERT, TOK_DEV * TOPK)
    pair_marks = (blocks[:, :, None] == jnp.arange(EXPERTS, dtype=jnp.int32)[None, None, :]).astype(jnp.int32)
    earlier = jnp.cumsum(pair_marks, axis=1) - pair_marks
    slot_index = lax.optimization_barrier(jnp.sum(earlier * pair_marks, axis=2))
    block_ids = jnp.arange(N_EXPERT, dtype=jnp.int32)[:, None]
    return (blocks * (N_EXPERT * CAP) + block_ids * CAP + slot_index).reshape(-1)

def reference(tokens_in, out_grad, routes, router, norm_gain, w_in, w_out):
    slot_total = EXPERTS * N_EXPERT * CAP
    row_shape = (EXPERTS, N_EXPERT * CAP, D)
    stored = []
    hidden_all = [tokens_in[micro_index] for micro_index in range(MICRO)]
    for layer_index in range(LAYERS):
        stored.append(hidden_all)
        new_all = []
        for micro_index in range(MICRO):
            hidden = hidden_all[micro_index]
            normed, scaled, inverse = normalize(hidden, norm_gain[layer_index])
            route_ids = routes[layer_index, micro_index]
            gate_probs, picked = router_gates(normed, router[layer_index], route_ids)
            positions = positions_of(route_ids)
            owners, filled = slot_owners(positions, slot_total)
            send_rows = to_slots(normed, owners // TOPK, filled, row_shape)
            produced = lax.map(lambda packed: expert_forward(packed[0], packed[1], packed[2]), (send_rows, w_in[layer_index], w_out[layer_index]))
            pair_outputs = produced.reshape(slot_total, D)[positions].reshape(TOKENS, TOPK, D)
            new_all.append(combine(hidden, gate_probs, pair_outputs))
        hidden_all = new_all
    grads_all = [out_grad[micro_index] for micro_index in range(MICRO)]
    layer_grads_in = []
    layer_grads_out = []
    for layer_index in reversed(range(LAYERS)):
        total_in = jnp.zeros((EXPERTS, D, 2 * FW), jnp.float32)
        total_out = jnp.zeros((EXPERTS, FW, D), jnp.float32)
        lower_all = []
        for micro_index in range(MICRO):
            hidden = stored[layer_index][micro_index]
            upstream = grads_all[micro_index]
            normed, scaled, inverse = normalize(hidden, norm_gain[layer_index])
            route_ids = routes[layer_index, micro_index]
            gate_probs, picked = router_gates(normed, router[layer_index], route_ids)
            positions = positions_of(route_ids)
            owners, filled = slot_owners(positions, slot_total)
            send_rows = to_slots(normed, owners // TOPK, filled, row_shape)
            send_grad = to_slots(upstream, owners // TOPK, filled, row_shape)
            send_share = to_slots(gate_probs.astype(jnp.bfloat16).reshape(-1), owners, filled, (EXPERTS, N_EXPERT * CAP))
            rows_grad, share_grad, grad_in, grad_out = lax.map(lambda packed: expert_backward(packed[0], packed[1], packed[2], packed[3], packed[4]), (send_rows, send_grad, send_share, w_in[layer_index], w_out[layer_index]))
            total_in = total_in + grad_in
            total_out = total_out + grad_out
            pair_grads = rows_grad.reshape(slot_total, D)[positions].reshape(TOKENS, TOPK, D)
            share_round = lax.optimization_barrier(share_grad.astype(jnp.bfloat16))
            pair_shares = share_round.reshape(slot_total)[positions].reshape(TOKENS, TOPK)
            lower_all.append(token_backward(upstream, scaled, inverse, norm_gain[layer_index], router[layer_index], gate_probs, picked, pair_grads, pair_shares))
        grads_all = lower_all
        layer_grads_in.append(total_in)
        layer_grads_out.append(total_out)
    return (jnp.stack(layer_grads_in[::-1]).astype(jnp.bfloat16), jnp.stack(layer_grads_out[::-1]).astype(jnp.bfloat16))
```

```python
import functools

import jax
import jax.numpy as jnp
from jax import lax
from jax.experimental import pallas as pl
from jax.experimental.pallas import tpu as pltpu
from jax.sharding import PartitionSpec as P

epsilon = 1e-06
CAP = 3
GROUPS = 2
LANES = 128
F32 = jnp.float32
BF16 = jnp.bfloat16
MESH = pl.DeviceIdType.MESH
NT = (((1,), (1,)), ((), ()))


def wide(value):
    return jnp.broadcast_to(value, (value.shape[0], LANES))


def relay(
    stages,
    ranks,
    micros,
    tokens,
    tables,
    source,
    gain,
    column,
    w_in_any,
    w_out_any,
    normed_out,
    joined_out,
    act_out,
    scaled_out,
    w_in,
    w_out,
    flat,
    staging,
    home_f_in,
    home_b_in,
    home_f_out,
    home_b_out,
    land_f,
    land_b,
    leave_f,
    leave_b,
    hidden,
    gate_part,
    up_part,
    produced,
    prob_kept,
    inverse_kept,
    up_grad,
    mixed,
    sems,
    weight_sems,
):
    chunks = micros * GROUPS
    slots = ranks * CAP
    homes = ranks // GROUPS
    rows = homes * CAP
    width = hidden.shape[2]
    tiles = width // LANES
    inner = w_out.shape[0]
    stage = lax.axis_index("pipe")
    me = lax.axis_index("expert")
    last = stages - 1
    my_group = lax.rem(me, GROUPS)
    my_place = lax.div(me, GROUPS)

    load_in = pltpu.make_async_copy(w_in_any.at[0, 0], w_in, weight_sems.at[0])
    load_out = pltpu.make_async_copy(w_out_any.at[0, 0], w_out, weight_sems.at[1])
    load_in.start()
    load_out.start()
    staging[slots] = jnp.zeros(staging.shape[1:], BF16)

    def drain(ref, sem):
        pltpu.make_async_copy(ref, ref, sem).wait()

    def home(chunk, table_row, at_source, came, came_sem, out, out_sem, land, land_sem):
        micro = lax.div(chunk, GROUPS)

        @pl.when(at_source)
        def _():
            staging[0:tokens] = source[micro]

        @pl.when(jnp.logical_not(at_source))
        def _():
            drain(came.at[micro], came_sem.at[micro])
            staging[0:slots] = came[micro]

        base = (table_row * micros + micro) * slots

        def place(step, carry):
            for inside in range(CAP):
                slot = step * CAP + inside
                out[micro, slot] = staging[tables[base + slot]]
            return carry

        lax.fori_loop(0, ranks, place, 0)
        mine = land.at[chunk, pl.ds(my_place * CAP, CAP)]
        pltpu.make_async_copy(
            out.at[micro, pl.ds(me * CAP, CAP)], mine, land_sem.at[chunk]
        ).start()

        def send(step, carry):
            peer = lax.rem(me + step, ranks)
            pltpu.make_async_remote_copy(
                src_ref=out.at[micro, pl.ds(peer * CAP, CAP)],
                dst_ref=mine,
                send_sem=out_sem.at[micro],
                recv_sem=land_sem.at[chunk],
                device_id={"pipe": stage, "expert": peer},
                device_id_type=MESH,
            ).start()
            return carry

        lax.fori_loop(1, ranks, send, 0)

    def send_home(chunk, to_stage, leave, leave_sem, came, came_sem):
        micro = lax.div(chunk, GROUPS)
        group = lax.rem(chunk, GROUPS)

        def send(step, carry):
            place = lax.rem(my_place + step, homes)
            pltpu.make_async_remote_copy(
                src_ref=leave.at[chunk, pl.ds(place * CAP, CAP)],
                dst_ref=came.at[micro, pl.ds(me * CAP, CAP)],
                send_sem=leave_sem.at[chunk],
                recv_sem=came_sem.at[micro],
                device_id={"pipe": to_stage, "expert": place * GROUPS + group},
                device_id_type=MESH,
            ).start()
            return carry

        lax.fori_loop(0, homes, send, 0)

    def spread(chunk, land):
        flat[...] = land[chunk].astype(F32).reshape(rows * tiles, LANES)

    def gather_rows(chunk, leave):
        leave[chunk] = flat[...].reshape(rows, tiles, LANES).astype(BF16)

    def strip(at):
        return pl.ds(at * LANES, LANES)

    def tile_rows(at):
        return pl.ds(at, rows, stride=tiles)

    def forward(chunk):
        drain(land_f.at[chunk], sems.at[1].at[chunk])
        spread(chunk, land_f)
        squares = jnp.zeros((rows, LANES), F32)
        for at in range(tiles):
            piece = flat[tile_rows(at), :]
            hidden[chunk, :, strip(at)] = piece
            squares += piece * piece
        inverse = lax.rsqrt(jnp.sum(squares, axis=1, keepdims=True) / width + epsilon)
        inverse = wide(inverse)
        inverse_kept[chunk] = inverse
        scores = jnp.zeros((rows, LANES), F32)
        for at in range(tiles):
            piece = hidden[chunk, :, strip(at)] * inverse * gain[:, strip(at)]
            piece = piece.astype(BF16)
            normed_out[chunk, :, strip(at)] = piece
            scores += piece.astype(F32) * column[:, strip(at)]
        prob = wide(jax.nn.sigmoid(jnp.sum(scores, axis=1, keepdims=True)))
        prob_kept[chunk] = prob
        share = prob.astype(BF16).astype(F32)
        normed = normed_out[chunk]
        block = min(256, inner)
        for at in range(inner // block):
            cols = pl.ds(at * block, block)
            g = jnp.dot(normed, w_in[:, cols], preferred_element_type=F32)
            u = jnp.dot(
                normed, w_in[:, pl.ds(inner + at * block, block)], preferred_element_type=F32
            )
            gate_part[chunk, :, cols] = g
            up_part[chunk, :, cols] = u
            act_out[chunk, :, cols] = (g * jax.nn.sigmoid(g) * u).astype(BF16)
        activated = act_out[chunk]
        block = min(256, width)
        for at in range(width // block):
            cols = pl.ds(at * block, block)
            result = jnp.dot(activated, w_out[:, cols], preferred_element_type=F32).astype(BF16)
            produced[chunk, :, cols] = result
            for inside in range(block // LANES):
                tile = at * (block // LANES) + inside
                piece = result[:, inside * LANES : (inside + 1) * LANES].astype(F32)
                flat[tile_rows(tile), :] = hidden[chunk, :, strip(tile)] + share * piece

        @pl.when(stage < last)
        def _():
            gather_rows(chunk, leave_f)
            send_home(chunk, stage + 1, leave_f, sems.at[2], home_f_in, sems.at[0])

    def backward(chunk):
        drain(land_b.at[chunk], sems.at[5].at[chunk])
        spread(chunk, land_b)
        prob = prob_kept[chunk]
        share = prob.astype(BF16).astype(F32)
        sums = jnp.zeros((rows, LANES), F32)
        for at in range(tiles):
            piece = flat[tile_rows(at), :]
            up_grad[:, strip(at)] = piece
            sums += produced[chunk, :, strip(at)].astype(F32) * piece
            scaled_out[chunk, :, strip(at)] = (share * piece).astype(BF16)
        share_grad = jnp.sum(sums, axis=1, keepdims=True).astype(BF16).astype(F32)
        logit_grad = wide(share_grad) * prob * (1.0 - prob)
        scaled_grad = scaled_out[chunk]
        block = min(256, inner)
        for at in range(inner // block):
            cols = pl.ds(at * block, block)
            act_grad = lax.dot_general(scaled_grad, w_out[cols, :], NT, preferred_element_type=F32)
            g = gate_part[chunk, :, cols]
            u = up_part[chunk, :, cols]
            s = jax.nn.sigmoid(g)
            joined_out[chunk, :, cols] = (act_grad * u * s * (1.0 + g * (1.0 - s))).astype(BF16)
            joined_out[chunk, :, pl.ds(inner + at * block, block)] = (act_grad * (g * s)).astype(
                BF16
            )

        @pl.when(stage > 0)
        def _():
            joined = joined_out[chunk]
            inverse = inverse_kept[chunk]
            wide_block = min(256, width)
            total = jnp.zeros((rows, LANES), F32)
            for at in range(width // wide_block):
                cols = pl.ds(at * wide_block, wide_block)
                result = lax.dot_general(joined, w_in[cols, :], NT, preferred_element_type=F32)
                for inside in range(wide_block // LANES):
                    tile = at * (wide_block // LANES) + inside
                    piece = result[:, inside * LANES : (inside + 1) * LANES]
                    piece = piece.astype(BF16).astype(F32) + logit_grad * column[:, strip(tile)]
                    piece = piece * gain[:, strip(tile)]
                    mixed[:, strip(tile)] = piece
                    total += piece * (hidden[chunk, :, strip(tile)] * inverse)
            mean = wide(jnp.sum(total, axis=1, keepdims=True) / width)
            for at in range(tiles):
                scaled = hidden[chunk, :, strip(at)] * inverse
                centred = mixed[:, strip(at)] - scaled * mean
                flat[tile_rows(at), :] = up_grad[:, strip(at)] + inverse * centred
            gather_rows(chunk, leave_b)
            send_home(chunk, stage - 1, leave_b, sems.at[6], home_b_in, sems.at[4])

    is_last = stage == last

    def step(turn, carry):
        @pl.when((turn < chunks) & (lax.rem(turn, GROUPS) == my_group))
        def _():
            home(
                turn, 0, stage == 0, home_f_in, sems.at[0],
                home_f_out, sems.at[3], land_f, sems.at[1],
            )

        @pl.when(turn == 1)
        def _():
            load_in.wait()
            load_out.wait()

        @pl.when((turn >= 1) & (turn <= chunks))
        def _():
            forward(turn - 1)

        back = jnp.where(is_last, turn, turn - chunks)

        @pl.when((back >= 0) & (back < chunks) & (lax.rem(back + chunks, GROUPS) == my_group))
        def _():
            home(
                back, 1, is_last, home_b_in, sems.at[4],
                home_b_out, sems.at[7], land_b, sems.at[5],
            )

        @pl.when((back >= 1) & (back <= chunks))
        def _():
            backward(back - 1)

        return carry

    lax.fori_loop(0, 2 * chunks + 1, step, 0)

    for micro in range(micros):
        away = pl.ds(0, slots - CAP)
        drain(home_f_out.at[micro, away], sems.at[3].at[micro])
        drain(home_b_out.at[micro, away], sems.at[7].at[micro])

    @pl.when(stage < last)
    def _():
        for chunk in range(chunks):
            drain(leave_f.at[chunk], sems.at[2].at[chunk])

    @pl.when(stage > 0)
    def _():
        for chunk in range(chunks):
            drain(leave_b.at[chunk], sems.at[6].at[chunk])


def row_tables(routes, stage, stages, slots):
    ids = routes[..., 0]

    def positions(layer):
        own = lax.dynamic_index_in_dim(ids, layer, 0, keepdims=False)
        order = jnp.arange(own.shape[1], dtype=jnp.int32)
        before = order[:, None] > order[None, :]
        same = (own[:, :, None] == own[:, None, :]) & before[None]
        return own * CAP + jnp.sum(same.astype(jnp.int32), axis=2)

    here = positions(stage)
    token = jnp.broadcast_to(jnp.arange(here.shape[1], dtype=jnp.int32)[None], here.shape)
    below = jnp.where(stage == 0, token, positions(jnp.maximum(stage - 1, 0)))
    above = jnp.where(stage == stages - 1, token, positions(jnp.minimum(stage + 1, stages - 1)))
    places = jnp.arange(slots, dtype=jnp.int32)
    hit = here[:, :, None] == places[None, None, :]
    pairs = jnp.stack([below, above])
    table = slots + jnp.sum(jnp.where(hit[None], pairs[..., None] - slots, 0), axis=2)
    return table.reshape(-1)


def weight_grad(left, right):
    dims = (((0, 1), (0, 1)), ((), ()))
    return lax.dot_general(left, right, dims, preferred_element_type=F32).astype(BF16)[None, None]


def shards(tokens_in, out_grad, routes, router, norm_gain, w_in, w_out):
    stages = lax.axis_size("pipe")
    ranks = lax.axis_size("expert")
    stage = lax.axis_index("pipe")
    me = lax.axis_index("expert")
    micros, tokens, width = tokens_in.shape
    inner = w_out.shape[2]
    tiles = width // LANES
    slots = ranks * CAP
    chunks = micros * GROUPS
    rows = slots // GROUPS
    source = jnp.where(stage == stages - 1, out_grad, tokens_in)
    source = source.reshape(micros, tokens, tiles, LANES)
    tables = row_tables(routes, stage, stages, slots)
    chosen = (jnp.arange(ranks, dtype=jnp.int32) == me).astype(BF16)[None]
    column = lax.dot_general(chosen, router[0], NT, preferred_element_type=F32)
    gain = norm_gain.astype(F32)

    vmem = pl.BlockSpec(memory_space=pltpu.VMEM)
    anywhere = pl.BlockSpec(memory_space=pl.ANY)
    parts = pl.pallas_call(
        functools.partial(relay, stages, ranks, micros, tokens),
        out_shape=(
            jax.ShapeDtypeStruct((chunks, rows, width), BF16),
            jax.ShapeDtypeStruct((chunks, rows, 2 * inner), BF16),
            jax.ShapeDtypeStruct((chunks, rows, inner), BF16),
            jax.ShapeDtypeStruct((chunks, rows, width), BF16),
        ),
        in_specs=[
            pl.BlockSpec(memory_space=pltpu.SMEM), vmem, vmem, vmem, anywhere, anywhere,
        ],
        out_specs=(vmem, vmem, vmem, vmem),
        scratch_shapes=[
            pltpu.VMEM((width, 2 * inner), BF16),
            pltpu.VMEM((inner, width), BF16),
            pltpu.VMEM((rows * tiles, LANES), F32),
            pltpu.VMEM((slots + 1, tiles, LANES), BF16),
            *[pltpu.VMEM((micros, slots, tiles, LANES), BF16)] * 4,
            *[pltpu.VMEM((chunks, rows, tiles, LANES), BF16)] * 4,
            pltpu.VMEM((chunks, rows, width), F32),
            pltpu.VMEM((chunks, rows, inner), F32),
            pltpu.VMEM((chunks, rows, inner), F32),
            pltpu.VMEM((chunks, rows, width), BF16),
            pltpu.VMEM((chunks, rows, LANES), F32),
            pltpu.VMEM((chunks, rows, LANES), F32),
            pltpu.VMEM((rows, width), F32),
            pltpu.VMEM((rows, width), F32),
            pltpu.SemaphoreType.DMA((8, chunks)),
            pltpu.SemaphoreType.DMA((2,)),
        ],
        compiler_params=pltpu.CompilerParams(
            has_side_effects=True, vmem_limit_bytes=56 * 1024 * 1024
        ),
        name="relay",
    )(tables, source, gain, column, w_in, w_out)
    normed, joined, activated, scaled = parts
    return (weight_grad(normed, joined), weight_grad(activated, scaled))


def solution(mesh):
    placed = (
        P(None, "expert", None),
        P(None, "expert", None),
        P(None, None, "expert", None),
        P("pipe", None, None),
        P("pipe", None),
        P("pipe", "expert", None, None),
        P("pipe", "expert", None, None),
    )
    return jax.shard_map(
        shards,
        mesh=mesh,
        in_specs=placed,
        out_specs=(P("pipe", "expert", None, None), P("pipe", "expert", None, None)),
        check_vma=False,
    )
```

```python
import functools

import jax
import jax.numpy as jnp
from jax import lax
from jax.experimental import pallas as pl
from jax.experimental.pallas import tpu as pltpu
from jax.sharding import PartitionSpec as P

epsilon = 1e-06
CAP = 3
GROUPS = 4
PACE = 8
LANES = 128
F32 = jnp.float32
BF16 = jnp.bfloat16
MESH = pl.DeviceIdType.MESH
NT = (((1,), (1,)), ((), ()))


def wide(value):
    return jnp.broadcast_to(value, (value.shape[0], LANES))


def relay(
    stages,
    ranks,
    micros,
    tokens,
    tables,
    source,
    gain_given,
    column,
    w_in_any,
    w_out_any,
    normed_out,
    joined_out,
    act_out,
    scaled_out,
    w_in,
    w_out,
    flat,
    staging,
    home_f_in,
    home_b_in,
    home_f_out,
    home_b_out,
    land_f,
    land_b,
    leave_f,
    leave_b,
    hidden,
    gate_part,
    up_part,
    produced,
    prob_kept,
    inverse_kept,
    up_grad,
    mixed,
    gain,
    sems,
    weight_sems,
):
    chunks = micros * GROUPS
    slots = ranks * CAP
    homes = ranks // GROUPS
    rows = homes * CAP
    width = hidden.shape[2]
    tiles = width // LANES
    inner = w_out.shape[0]
    stage = lax.axis_index("pipe")
    me = lax.axis_index("expert")
    last = stages - 1
    my_group = lax.rem(me, GROUPS)
    my_place = lax.div(me, GROUPS)

    load_in = pltpu.make_async_copy(w_in_any.at[0, 0], w_in, weight_sems.at[0])
    load_out = pltpu.make_async_copy(w_out_any.at[0, 0], w_out, weight_sems.at[1])
    load_in.start()
    load_out.start()
    staging[slots] = jnp.zeros(staging.shape[1:], BF16)

    ring = ranks // 4
    my_ring = lax.rem(lax.div(me, 2), ring)

    def neighbour(step, inside):
        half = lax.div(step + 1, 2)
        away = jnp.where(lax.rem(step, 2) == 1, ring // 2 + half, ring // 2 + ring - half)
        side = lax.rem(lax.div(me, 2 * ring) + inside // 2, 2)
        core = lax.rem(me + inside, 2)
        return (side * ring + lax.rem(my_ring + away, ring)) * 2 + core

    gain[...] = gain_given[...].astype(F32)

    def drain(ref, sem):
        pltpu.make_async_copy(ref, ref, sem).wait()

    def home(
        chunk, table_row, to_stage, at_source, pace, came, came_sem, out, out_sem, land, land_sem
    ):
        micro = lax.div(chunk, GROUPS)

        @pl.when(at_source)
        def _():
            staging[0:tokens] = source[micro]

        @pl.when(jnp.logical_not(at_source))
        def _():
            drain(came.at[micro], came_sem.at[micro])
            staging[0:slots] = came[micro]

        base = (table_row * micros + micro) * slots

        def place(step, carry):
            for inside in range(CAP):
                slot = step * CAP + inside
                out[micro, slot] = staging[tables[base + slot]]
            return carry

        def again(step, carry):
            lax.fori_loop(0, ranks, place, 0)
            return carry

        lead = jnp.where(chunk < GROUPS, chunk, GROUPS)
        lax.fori_loop(0, jnp.where(at_source, 1 + pace * lead, 1), again, 0)
        mine = land.at[chunk, pl.ds(my_place * CAP, CAP)]

        def send(step, carry):
            for inside in (3, 2, 1, 0):
                peer = neighbour(step, inside)
                pltpu.make_async_remote_copy(
                    src_ref=out.at[micro, pl.ds(peer * CAP, CAP)],
                    dst_ref=mine,
                    send_sem=out_sem.at[micro],
                    recv_sem=land_sem.at[chunk],
                    device_id={"pipe": to_stage, "expert": peer},
                    device_id_type=MESH,
                ).start()
            return carry

        lax.fori_loop(0, ring, send, 0)

    def send_home(chunk, to_stage, leave, leave_sem, came, came_sem):
        micro = lax.div(chunk, GROUPS)
        group = lax.rem(chunk, GROUPS)

        zs = homes // 2

        def send(step, carry):
            half = lax.div(step + 1, 2)
            away = jnp.where(lax.rem(step, 2) == 1, zs // 2 + half, zs // 2 + zs - half)
            z = lax.rem(lax.rem(my_place, zs) + away, zs)
            for inside in (1, 0):
                place = lax.rem(lax.div(my_place, zs) + inside, 2) * zs + z
                pltpu.make_async_remote_copy(
                    src_ref=leave.at[chunk, pl.ds(place * CAP, CAP)],
                    dst_ref=came.at[micro, pl.ds(me * CAP, CAP)],
                    send_sem=leave_sem.at[chunk],
                    recv_sem=came_sem.at[micro],
                    device_id={"pipe": to_stage, "expert": place * GROUPS + group},
                    device_id_type=MESH,
                ).start()
            return carry

        lax.fori_loop(0, zs, send, 0)

    def spread(chunk, land):
        flat[...] = land[chunk].astype(F32).reshape(rows * tiles, LANES)

    def gather_rows(chunk, leave):
        leave[chunk] = flat[...].reshape(rows, tiles, LANES).astype(BF16)

    def strip(at):
        return pl.ds(at * LANES, LANES)

    def tile_rows(at):
        return pl.ds(at, rows, stride=tiles)

    def forward(chunk):
        drain(land_f.at[chunk], sems.at[1].at[chunk])
        spread(chunk, land_f)
        squares = jnp.zeros((rows, LANES), F32)
        for at in range(tiles):
            piece = flat[tile_rows(at), :]
            hidden[chunk, :, strip(at)] = piece
            squares += piece * piece
        inverse = lax.rsqrt(jnp.sum(squares, axis=1, keepdims=True) / width + epsilon)
        inverse = wide(inverse)
        inverse_kept[chunk] = inverse
        scores = jnp.zeros((rows, LANES), F32)
        for at in range(tiles):
            piece = hidden[chunk, :, strip(at)] * inverse * gain[:, strip(at)]
            piece = piece.astype(BF16)
            normed_out[chunk, :, strip(at)] = piece
            scores += piece.astype(F32) * column[:, strip(at)]
        prob = wide(jax.nn.sigmoid(jnp.sum(scores, axis=1, keepdims=True)))
        prob_kept[chunk] = prob
        share = prob.astype(BF16).astype(F32)
        normed = normed_out[chunk]
        block = min(256, inner)
        for at in range(inner // block):
            cols = pl.ds(at * block, block)
            g = jnp.dot(normed, w_in[:, cols], preferred_element_type=F32)
            u = jnp.dot(
                normed, w_in[:, pl.ds(inner + at * block, block)], preferred_element_type=F32
            )
            gate_part[chunk, :, cols] = g
            up_part[chunk, :, cols] = u
            act_out[chunk, :, cols] = (g * jax.nn.sigmoid(g) * u).astype(BF16)
        activated = act_out[chunk]
        block = min(256, width)
        for at in range(width // block):
            cols = pl.ds(at * block, block)
            result = jnp.dot(activated, w_out[:, cols], preferred_element_type=F32).astype(BF16)
            produced[chunk, :, cols] = result
            for inside in range(block // LANES):
                tile = at * (block // LANES) + inside
                piece = result[:, inside * LANES : (inside + 1) * LANES].astype(F32)
                flat[tile_rows(tile), :] = hidden[chunk, :, strip(tile)] + share * piece

        @pl.when(stage < last)
        def _():
            gather_rows(chunk, leave_f)
            send_home(chunk, lax.rem(stage + 2, stages), leave_f, sems.at[2], home_f_in, sems.at[0])

    def backward(chunk):
        drain(land_b.at[chunk], sems.at[5].at[chunk])
        spread(chunk, land_b)
        prob = prob_kept[chunk]
        share = prob.astype(BF16).astype(F32)
        sums = jnp.zeros((rows, LANES), F32)
        for at in range(tiles):
            piece = flat[tile_rows(at), :]
            up_grad[:, strip(at)] = piece
            sums += produced[chunk, :, strip(at)].astype(F32) * piece
            scaled_out[chunk, :, strip(at)] = (share * piece).astype(BF16)
        share_grad = jnp.sum(sums, axis=1, keepdims=True).astype(BF16).astype(F32)
        logit_grad = wide(share_grad) * prob * (1.0 - prob)
        scaled_grad = scaled_out[chunk]
        block = min(256, inner)
        for at in range(inner // block):
            cols = pl.ds(at * block, block)
            act_grad = lax.dot_general(scaled_grad, w_out[cols, :], NT, preferred_element_type=F32)
            g = gate_part[chunk, :, cols]
            u = up_part[chunk, :, cols]
            s = jax.nn.sigmoid(g)
            joined_out[chunk, :, cols] = (act_grad * u * s * (1.0 + g * (1.0 - s))).astype(BF16)
            joined_out[chunk, :, pl.ds(inner + at * block, block)] = (act_grad * (g * s)).astype(
                BF16
            )

        @pl.when(stage > 0)
        def _():
            joined = joined_out[chunk]
            inverse = inverse_kept[chunk]
            wide_block = min(256, width)
            total = jnp.zeros((rows, LANES), F32)
            for at in range(width // wide_block):
                cols = pl.ds(at * wide_block, wide_block)
                result = lax.dot_general(joined, w_in[cols, :], NT, preferred_element_type=F32)
                for inside in range(wide_block // LANES):
                    tile = at * (wide_block // LANES) + inside
                    piece = result[:, inside * LANES : (inside + 1) * LANES]
                    piece = piece.astype(BF16).astype(F32) + logit_grad * column[:, strip(tile)]
                    piece = piece * gain[:, strip(tile)]
                    mixed[:, strip(tile)] = piece
                    total += piece * (hidden[chunk, :, strip(tile)] * inverse)
            mean = wide(jnp.sum(total, axis=1, keepdims=True) / width)
            for at in range(tiles):
                scaled = hidden[chunk, :, strip(at)] * inverse
                centred = mixed[:, strip(at)] - scaled * mean
                flat[tile_rows(at), :] = up_grad[:, strip(at)] + inverse * centred
            gather_rows(chunk, leave_b)
            send_home(chunk, lax.rem(stage + stages - 2, stages), leave_b, sems.at[6], home_b_in, sems.at[4])

    is_last = stage == last

    serve_f = jnp.where(stage == 0, 2 * chunks, 0)
    serve_b = jnp.where(stage == last - 1, 0, jnp.where(is_last, 4 * chunks, 3 * chunks))
    run_b = jnp.where(is_last, chunks, 4 * chunks)
    next_f = lax.rem(stage + stages - 1, stages)
    next_b = lax.rem(stage + 1, stages)

    def within(at):
        return (at >= 0) & (at < chunks)

    def served(at):
        return within(at) & (lax.rem(at + 4 * chunks, GROUPS) == my_group)

    def step(turn, carry):
        @pl.when(served(turn - serve_b))
        def _():
            home(
                turn - serve_b, 1, next_b, next_b == last, 0, home_b_in, sems.at[4],
                home_b_out, sems.at[7], land_b, sems.at[5],
            )

        @pl.when(served(turn - serve_f))
        def _():
            home(
                turn - serve_f, 0, next_f, next_f == 0, PACE, home_f_in, sems.at[0],
                home_f_out, sems.at[3], land_f, sems.at[1],
            )

        @pl.when(turn == chunks)
        def _():
            load_in.wait()
            load_out.wait()

        @pl.when(within(turn - chunks))
        def _():
            forward(turn - chunks)

        @pl.when(within(turn - run_b))
        def _():
            backward(turn - run_b)

        return carry

    lax.fori_loop(0, 5 * chunks, step, 0)

    for micro in range(micros):
        drain(home_f_out.at[micro], sems.at[3].at[micro])
        drain(home_b_out.at[micro], sems.at[7].at[micro])

    @pl.when(stage < last)
    def _():
        for chunk in range(chunks):
            drain(leave_f.at[chunk], sems.at[2].at[chunk])

    @pl.when(stage > 0)
    def _():
        for chunk in range(chunks):
            drain(leave_b.at[chunk], sems.at[6].at[chunk])


def row_tables(routes, stage, stages, slots):
    ids = routes[..., 0]
    order = jnp.arange(ids.shape[2], dtype=jnp.int32)
    before = order[:, None] > order[None, :]
    same = (ids[..., :, None] == ids[..., None, :]) & before
    positions = ids * CAP + jnp.sum(same.astype(jnp.int32), axis=3)

    def layer(index):
        return lax.dynamic_index_in_dim(positions, jnp.clip(index, 0, stages - 1), 0, False)

    to_f = lax.rem(stage + stages - 1, stages)
    to_b = lax.rem(stage + 1, stages)
    token = jnp.broadcast_to(order[None], ids.shape[1:])
    here = jnp.stack([layer(to_f), layer(to_b)])
    there = jnp.stack(
        [
            jnp.where(to_f == 0, token, layer(to_f - 1)),
            jnp.where(to_b == stages - 1, token, layer(to_b + 1)),
        ]
    )
    hit = here[..., None] == jnp.arange(slots, dtype=jnp.int32)
    table = slots + jnp.sum(jnp.where(hit, there[..., None] - slots, 0), axis=2)
    return table.reshape(-1)


def weight_grad(left, right):
    dims = (((0, 1), (0, 1)), ((), ()))
    return lax.dot_general(left, right, dims, preferred_element_type=F32).astype(BF16)[None, None]


def shards(tokens_in, out_grad, routes, router, norm_gain, w_in, w_out):
    stages = lax.axis_size("pipe")
    ranks = lax.axis_size("expert")
    stage = lax.axis_index("pipe")
    me = lax.axis_index("expert")
    micros, tokens, width = tokens_in.shape
    inner = w_out.shape[2]
    tiles = width // LANES
    slots = ranks * CAP
    chunks = micros * GROUPS
    rows = slots // GROUPS
    source = jnp.where(stage == stages - 2, out_grad, tokens_in)
    source = source.reshape(micros, tokens, tiles, LANES)
    tables = row_tables(routes, stage, stages, slots)
    chosen = (jnp.arange(ranks, dtype=jnp.int32) == me).astype(BF16)[None]
    column = lax.dot_general(chosen, router[0], NT, preferred_element_type=F32)

    vmem = pl.BlockSpec(memory_space=pltpu.VMEM)
    anywhere = pl.BlockSpec(memory_space=pl.ANY)
    parts = pl.pallas_call(
        functools.partial(relay, stages, ranks, micros, tokens),
        out_shape=(
            jax.ShapeDtypeStruct((chunks, rows, width), BF16),
            jax.ShapeDtypeStruct((chunks, rows, 2 * inner), BF16),
            jax.ShapeDtypeStruct((chunks, rows, inner), BF16),
            jax.ShapeDtypeStruct((chunks, rows, width), BF16),
        ),
        in_specs=[
            pl.BlockSpec(memory_space=pltpu.SMEM), vmem, vmem, vmem, anywhere, anywhere,
        ],
        out_specs=(vmem, vmem, vmem, vmem),
        scratch_shapes=[
            pltpu.VMEM((width, 2 * inner), BF16),
            pltpu.VMEM((inner, width), BF16),
            pltpu.VMEM((rows * tiles, LANES), F32),
            pltpu.VMEM((slots + 1, tiles, LANES), BF16),
            *[pltpu.VMEM((micros, slots, tiles, LANES), BF16)] * 4,
            *[pltpu.VMEM((chunks, rows, tiles, LANES), BF16)] * 4,
            pltpu.VMEM((chunks, rows, width), F32),
            pltpu.VMEM((chunks, rows, inner), F32),
            pltpu.VMEM((chunks, rows, inner), F32),
            pltpu.VMEM((chunks, rows, width), BF16),
            pltpu.VMEM((chunks, rows, LANES), F32),
            pltpu.VMEM((chunks, rows, LANES), F32),
            pltpu.VMEM((rows, width), F32),
            pltpu.VMEM((rows, width), F32),
            pltpu.VMEM((1, width), F32),
            pltpu.SemaphoreType.DMA((8, chunks)),
            pltpu.SemaphoreType.DMA((2,)),
        ],
        compiler_params=pltpu.CompilerParams(
            has_side_effects=True, vmem_limit_bytes=56 * 1024 * 1024
        ),
        name="relay",
    )(tables, source, norm_gain, column, w_in, w_out)
    normed, joined, activated, scaled = parts
    return (weight_grad(normed, joined), weight_grad(activated, scaled))


def solution(mesh):
    placed = (
        P(None, "expert", None),
        P(None, "expert", None),
        P(None, None, "expert", None),
        P("pipe", None, None),
        P("pipe", None),
        P("pipe", "expert", None, None),
        P("pipe", "expert", None, None),
    )
    return jax.shard_map(
        shards,
        mesh=mesh,
        in_specs=placed,
        out_specs=(P("pipe", "expert", None, None), P("pipe", "expert", None, None)),
        check_vma=False,
    )
```

```python
import functools

import jax
import jax.numpy as jnp
from jax import lax
from jax.experimental import pallas as pl
from jax.experimental.pallas import tpu as pltpu
from jax.sharding import PartitionSpec as P

epsilon = 1e-06
CAP = 3
GROUPS = 4
PACE = 12
LANES = 128
F32 = jnp.float32
BF16 = jnp.bfloat16
MESH = pl.DeviceIdType.MESH
NT = (((1,), (1,)), ((), ()))


def wide(value):
    return jnp.broadcast_to(value, (value.shape[0], LANES))


def relay(
    stages,
    ranks,
    micros,
    tokens,
    tables,
    source,
    gain_given,
    column,
    w_in_any,
    w_out_any,
    normed_out,
    joined_out,
    act_out,
    scaled_out,
    w_in,
    w_out,
    flat,
    staging,
    home_f_in,
    home_b_in,
    home_f_out,
    home_b_out,
    land_f,
    land_b,
    leave_f,
    leave_b,
    hidden,
    gate_part,
    up_part,
    produced,
    prob_kept,
    inverse_kept,
    up_grad,
    mixed,
    gain,
    sems,
    weight_sems,
):
    chunks = micros * GROUPS
    slots = ranks * CAP
    homes = ranks // GROUPS
    rows = homes * CAP
    width = hidden.shape[2]
    tiles = width // LANES
    inner = w_out.shape[0]
    stage = lax.axis_index("pipe")
    me = lax.axis_index("expert")
    last = stages - 1
    my_group = lax.rem(me, GROUPS)
    my_place = lax.div(me, GROUPS)

    load_in = pltpu.make_async_copy(w_in_any.at[0, 0], w_in, weight_sems.at[0])
    load_out = pltpu.make_async_copy(w_out_any.at[0, 0], w_out, weight_sems.at[1])
    load_in.start()
    load_out.start()
    staging[slots] = jnp.zeros(staging.shape[1:], BF16)

    ring = ranks // 4
    my_ring = lax.rem(lax.div(me, 2), ring)

    def neighbour(step, inside):
        half = lax.div(step + 1, 2)
        away = jnp.where(lax.rem(step, 2) == 1, ring // 2 + half, ring // 2 + ring - half)
        side = lax.rem(lax.div(me, 2 * ring) + inside // 2, 2)
        core = lax.rem(me + inside, 2)
        return (side * ring + lax.rem(my_ring + away, ring)) * 2 + core

    gain[...] = gain_given[...].astype(F32)

    def drain(ref, sem):
        pltpu.make_async_copy(ref, ref, sem).wait()

    def home(
        chunk, table_row, to_stage, at_source, pace, came, came_sem, out, out_sem, land, land_sem
    ):
        micro = lax.div(chunk, GROUPS)

        @pl.when(at_source)
        def _():
            staging[0:tokens] = source[micro]

        @pl.when(jnp.logical_not(at_source))
        def _():
            drain(came.at[micro], came_sem.at[micro])
            staging[0:slots] = came[micro]

        base = (table_row * micros + micro) * slots

        def place(step, carry):
            for inside in range(4 * CAP):
                slot = step * (4 * CAP) + inside
                out[micro, slot] = staging[tables[base + slot]]
            return carry

        def again(step, carry):
            lax.fori_loop(0, ranks // 4, place, 0)
            return carry

        lead = jnp.where(chunk < GROUPS, chunk, GROUPS)
        lax.fori_loop(0, jnp.where(at_source, 1 + pace * lead, 1), again, 0)
        mine = land.at[chunk, pl.ds(my_place * CAP, CAP)]

        def send(step, carry):
            for inside in (3, 2, 1, 0):
                peer = neighbour(step, inside)
                pltpu.make_async_remote_copy(
                    src_ref=out.at[micro, pl.ds(peer * CAP, CAP)],
                    dst_ref=mine,
                    send_sem=out_sem.at[micro],
                    recv_sem=land_sem.at[chunk],
                    device_id={"pipe": to_stage, "expert": peer},
                    device_id_type=MESH,
                ).start()
            return carry

        lax.fori_loop(0, ring, send, 0)

    def send_home(chunk, to_stage, leave, leave_sem, came, came_sem):
        micro = lax.div(chunk, GROUPS)
        group = lax.rem(chunk, GROUPS)

        zs = homes // 2

        def send(step, carry):
            half = lax.div(step + 1, 2)
            away = jnp.where(lax.rem(step, 2) == 1, zs // 2 + half, zs // 2 + zs - half)
            z = lax.rem(lax.rem(my_place, zs) + away, zs)
            for inside in (1, 0):
                place = lax.rem(lax.div(my_place, zs) + inside, 2) * zs + z
                pltpu.make_async_remote_copy(
                    src_ref=leave.at[chunk, pl.ds(place * CAP, CAP)],
                    dst_ref=came.at[micro, pl.ds(me * CAP, CAP)],
                    send_sem=leave_sem.at[chunk],
                    recv_sem=came_sem.at[micro],
                    device_id={"pipe": to_stage, "expert": place * GROUPS + group},
                    device_id_type=MESH,
                ).start()
            return carry

        lax.fori_loop(0, zs, send, 0)

    def spread(chunk, land):
        flat[...] = land[chunk].astype(F32).reshape(rows * tiles, LANES)

    def gather_rows(chunk, leave):
        leave[chunk] = flat[...].reshape(rows, tiles, LANES).astype(BF16)

    def strip(at):
        return pl.ds(at * LANES, LANES)

    def tile_rows(at):
        return pl.ds(at, rows, stride=tiles)

    def forward(chunk):
        drain(land_f.at[chunk], sems.at[1].at[chunk])
        spread(chunk, land_f)
        squares = jnp.zeros((rows, LANES), F32)
        for at in range(tiles):
            piece = flat[tile_rows(at), :]
            hidden[chunk, :, strip(at)] = piece
            squares += piece * piece
        inverse = lax.rsqrt(jnp.sum(squares, axis=1, keepdims=True) / width + epsilon)
        inverse = wide(inverse)
        inverse_kept[chunk] = inverse
        scores = jnp.zeros((rows, LANES), F32)
        for at in range(tiles):
            piece = hidden[chunk, :, strip(at)] * inverse * gain[:, strip(at)]
            piece = piece.astype(BF16)
            normed_out[chunk, :, strip(at)] = piece
            scores += piece.astype(F32) * column[:, strip(at)]
        prob = wide(jax.nn.sigmoid(jnp.sum(scores, axis=1, keepdims=True)))
        prob_kept[chunk] = prob
        share = prob.astype(BF16).astype(F32)
        normed = normed_out[chunk]
        block = min(256, inner)
        for at in range(inner // block):
            cols = pl.ds(at * block, block)
            g = jnp.dot(normed, w_in[:, cols], preferred_element_type=F32)
            u = jnp.dot(
                normed, w_in[:, pl.ds(inner + at * block, block)], preferred_element_type=F32
            )
            gate_part[chunk, :, cols] = g
            up_part[chunk, :, cols] = u
            act_out[chunk, :, cols] = (g * jax.nn.sigmoid(g) * u).astype(BF16)
        activated = act_out[chunk]
        block = min(256, width)
        for at in range(width // block):
            cols = pl.ds(at * block, block)
            result = jnp.dot(activated, w_out[:, cols], preferred_element_type=F32).astype(BF16)
            produced[chunk, :, cols] = result
            for inside in range(block // LANES):
                tile = at * (block // LANES) + inside
                piece = result[:, inside * LANES : (inside + 1) * LANES].astype(F32)
                flat[tile_rows(tile), :] = hidden[chunk, :, strip(tile)] + share * piece

        @pl.when(stage < last)
        def _():
            gather_rows(chunk, leave_f)
            send_home(chunk, lax.rem(stage + 2, stages), leave_f, sems.at[2], home_f_in, sems.at[0])

    def backward(chunk):
        drain(land_b.at[chunk], sems.at[5].at[chunk])
        spread(chunk, land_b)
        prob = prob_kept[chunk]
        share = prob.astype(BF16).astype(F32)
        sums = jnp.zeros((rows, LANES), F32)
        for at in range(tiles):
            piece = flat[tile_rows(at), :]
            up_grad[:, strip(at)] = piece
            sums += produced[chunk, :, strip(at)].astype(F32) * piece
            scaled_out[chunk, :, strip(at)] = (share * piece).astype(BF16)
        share_grad = jnp.sum(sums, axis=1, keepdims=True).astype(BF16).astype(F32)
        logit_grad = wide(share_grad) * prob * (1.0 - prob)
        scaled_grad = scaled_out[chunk]
        block = min(256, inner)
        for at in range(inner // block):
            cols = pl.ds(at * block, block)
            act_grad = lax.dot_general(scaled_grad, w_out[cols, :], NT, preferred_element_type=F32)
            g = gate_part[chunk, :, cols]
            u = up_part[chunk, :, cols]
            s = jax.nn.sigmoid(g)
            joined_out[chunk, :, cols] = (act_grad * u * s * (1.0 + g * (1.0 - s))).astype(BF16)
            joined_out[chunk, :, pl.ds(inner + at * block, block)] = (act_grad * (g * s)).astype(
                BF16
            )

        @pl.when(stage > 0)
        def _():
            joined = joined_out[chunk]
            inverse = inverse_kept[chunk]
            wide_block = min(256, width)
            total = jnp.zeros((rows, LANES), F32)
            for at in range(width // wide_block):
                cols = pl.ds(at * wide_block, wide_block)
                result = lax.dot_general(joined, w_in[cols, :], NT, preferred_element_type=F32)
                for inside in range(wide_block // LANES):
                    tile = at * (wide_block // LANES) + inside
                    piece = result[:, inside * LANES : (inside + 1) * LANES]
                    piece = piece.astype(BF16).astype(F32) + logit_grad * column[:, strip(tile)]
                    piece = piece * gain[:, strip(tile)]
                    mixed[:, strip(tile)] = piece
                    total += piece * (hidden[chunk, :, strip(tile)] * inverse)
            mean = wide(jnp.sum(total, axis=1, keepdims=True) / width)
            for at in range(tiles):
                scaled = hidden[chunk, :, strip(at)] * inverse
                centred = mixed[:, strip(at)] - scaled * mean
                flat[tile_rows(at), :] = up_grad[:, strip(at)] + inverse * centred
            gather_rows(chunk, leave_b)
            send_home(chunk, lax.rem(stage + stages - 2, stages), leave_b, sems.at[6], home_b_in, sems.at[4])

    is_last = stage == last

    serve_f = jnp.where(stage == 0, 2 * chunks, 0)
    serve_b = jnp.where(stage == last - 1, 0, jnp.where(is_last, 4 * chunks, 3 * chunks))
    run_b = jnp.where(is_last, chunks, 4 * chunks)
    next_f = lax.rem(stage + stages - 1, stages)
    next_b = lax.rem(stage + 1, stages)

    def within(at):
        return (at >= 0) & (at < chunks)

    def served(at):
        return within(at) & (lax.rem(at + 4 * chunks, GROUPS) == my_group)

    def step(turn, carry):
        @pl.when(served(turn - serve_b))
        def _():
            home(
                turn - serve_b, 1, next_b, next_b == last, 0, home_b_in, sems.at[4],
                home_b_out, sems.at[7], land_b, sems.at[5],
            )

        @pl.when(served(turn - serve_f))
        def _():
            home(
                turn - serve_f, 0, next_f, next_f == 0, PACE, home_f_in, sems.at[0],
                home_f_out, sems.at[3], land_f, sems.at[1],
            )

        @pl.when(turn == chunks)
        def _():
            load_in.wait()
            load_out.wait()

        @pl.when(within(turn - chunks))
        def _():
            forward(turn - chunks)

        @pl.when(within(turn - run_b))
        def _():
            backward(turn - run_b)

        return carry

    lax.fori_loop(0, 5 * chunks, step, 0)

    for micro in range(micros):
        drain(home_f_out.at[micro], sems.at[3].at[micro])
        drain(home_b_out.at[micro], sems.at[7].at[micro])

    @pl.when(stage < last)
    def _():
        for chunk in range(chunks):
            drain(leave_f.at[chunk], sems.at[2].at[chunk])

    @pl.when(stage > 0)
    def _():
        for chunk in range(chunks):
            drain(leave_b.at[chunk], sems.at[6].at[chunk])


def row_tables(routes, stage, stages, slots):
    ids = routes[..., 0]
    order = jnp.arange(ids.shape[2], dtype=jnp.int32)
    before = order[:, None] > order[None, :]
    same = (ids[..., :, None] == ids[..., None, :]) & before
    positions = ids * CAP + jnp.sum(same.astype(jnp.int32), axis=3)

    def layer(index):
        return lax.dynamic_index_in_dim(positions, jnp.clip(index, 0, stages - 1), 0, False)

    to_f = lax.rem(stage + stages - 1, stages)
    to_b = lax.rem(stage + 1, stages)
    token = jnp.broadcast_to(order[None], ids.shape[1:])
    here = jnp.stack([layer(to_f), layer(to_b)])
    there = jnp.stack(
        [
            jnp.where(to_f == 0, token, layer(to_f - 1)),
            jnp.where(to_b == stages - 1, token, layer(to_b + 1)),
        ]
    )
    hit = here[..., None] == jnp.arange(slots, dtype=jnp.int32)
    table = slots + jnp.sum(jnp.where(hit, there[..., None] - slots, 0), axis=2)
    return table.reshape(-1)


def weight_grad(left, right):
    dims = (((0, 1), (0, 1)), ((), ()))
    return lax.dot_general(left, right, dims, preferred_element_type=F32).astype(BF16)[None, None]


def shards(tokens_in, out_grad, routes, router, norm_gain, w_in, w_out):
    stages = lax.axis_size("pipe")
    ranks = lax.axis_size("expert")
    stage = lax.axis_index("pipe")
    me = lax.axis_index("expert")
    micros, tokens, width = tokens_in.shape
    inner = w_out.shape[2]
    tiles = width // LANES
    slots = ranks * CAP
    chunks = micros * GROUPS
    rows = slots // GROUPS
    source = jnp.where(stage == stages - 2, out_grad, tokens_in)
    source = source.reshape(micros, tokens, tiles, LANES)
    tables = row_tables(routes, stage, stages, slots)
    chosen = (jnp.arange(ranks, dtype=jnp.int32) == me).astype(BF16)[None]
    column = lax.dot_general(chosen, router[0], NT, preferred_element_type=F32)

    vmem = pl.BlockSpec(memory_space=pltpu.VMEM)
    anywhere = pl.BlockSpec(memory_space=pl.ANY)
    parts = pl.pallas_call(
        functools.partial(relay, stages, ranks, micros, tokens),
        out_shape=(
            jax.ShapeDtypeStruct((chunks, rows, width), BF16),
            jax.ShapeDtypeStruct((chunks, rows, 2 * inner), BF16),
            jax.ShapeDtypeStruct((chunks, rows, inner), BF16),
            jax.ShapeDtypeStruct((chunks, rows, width), BF16),
        ),
        in_specs=[
            pl.BlockSpec(memory_space=pltpu.SMEM), vmem, vmem, vmem, anywhere, anywhere,
        ],
        out_specs=(vmem, vmem, vmem, vmem),
        scratch_shapes=[
            pltpu.VMEM((width, 2 * inner), BF16),
            pltpu.VMEM((inner, width), BF16),
            pltpu.VMEM((rows * tiles, LANES), F32),
            pltpu.VMEM((slots + 1, tiles, LANES), BF16),
            *[pltpu.VMEM((micros, slots, tiles, LANES), BF16)] * 4,
            *[pltpu.VMEM((chunks, rows, tiles, LANES), BF16)] * 4,
            pltpu.VMEM((chunks, rows, width), F32),
            pltpu.VMEM((chunks, rows, inner), F32),
            pltpu.VMEM((chunks, rows, inner), F32),
            pltpu.VMEM((chunks, rows, width), BF16),
            pltpu.VMEM((chunks, rows, LANES), F32),
            pltpu.VMEM((chunks, rows, LANES), F32),
            pltpu.VMEM((rows, width), F32),
            pltpu.VMEM((rows, width), F32),
            pltpu.VMEM((1, width), F32),
            pltpu.SemaphoreType.DMA((8, chunks)),
            pltpu.SemaphoreType.DMA((2,)),
        ],
        compiler_params=pltpu.CompilerParams(
            has_side_effects=True, vmem_limit_bytes=56 * 1024 * 1024
        ),
        name="relay",
    )(tables, source, norm_gain, column, w_in, w_out)
    normed, joined, activated, scaled = parts
    return (weight_grad(normed, joined), weight_grad(activated, scaled))


def solution(mesh):
    placed = (
        P(None, "expert", None),
        P(None, "expert", None),
        P(None, None, "expert", None),
        P("pipe", None, None),
        P("pipe", None),
        P("pipe", "expert", None, None),
        P("pipe", "expert", None, None),
    )
    return jax.shard_map(
        shards,
        mesh=mesh,
        in_specs=placed,
        out_specs=(P("pipe", "expert", None, None), P("pipe", "expert", None, None)),
        check_vma=False,
    )
```
